768 devices in a mesh: leaf: 96 (over z, y), sub: 8 (over x, core).
Axes of the slice: x: 4, y: 8, z: 12, core: 2. Of those that a mesh axis runs over, the one named last changes fastest.
Arguments:
- start_vec: float32 [3072, 256], P(('leaf', 'sub')), as said below
- near_blocks: bfloat16 [3072, 2, 256, 256], P(('leaf', 'sub')), may hold values from -0.25 to 0.25
- near_ids: int32 [3072, 1], P(('leaf', 'sub')), may hold values from 0 to 95
- far_ids: int32 [3072, 2], P(('leaf', 'sub')), may hold values from 0 to 31
- leaf_basis: bfloat16 [3072, 64, 256], P(('leaf', 'sub')), may hold values from -0.375 to 0.375
- leaf_coupling: bfloat16 [3072, 64, 128], P(('leaf', 'sub')), may hold values from -0.5 to 0.5
- node_transfer: bfloat16 [768, 64, 256], P(('leaf', 'sub')), may hold values from -0.375 to 0.375
- branch_transfer: bfloat16 [768, 64, 64], P(('leaf', 'sub')), may hold values from -0.75 to 0.75
- top_ids: int32 [96, 4], P('leaf'), may hold values from 0 to 95
- top_coupling: bfloat16 [96, 64, 256], P('leaf'), may hold values from -0.375 to 0.375
Outputs:
- basis: float32 [4, 3072, 256], P(None, ('leaf', 'sub'))
- hessen: float32 [4, 3], replicated
The draws below stay inside these ranges and needn't reach their ends.
Inputs may be any that keep to these rules, and one draw needn't show every extreme that they name: start_vec is real-valued with entries of order one.
All inputs are finite; a program needn't handle non-finite values.
Results may differ from the reference program's by a relative error of at most 0.02.
Values may be sent and summed in bfloat16 or wider, within the bound.
A program may use at most 32 MiB of HBM per device.

```python
import jax
import jax.numpy as jnp
from jax import lax

LEAF = 256
RANK = 64
LEAVES_DEV = 4
NEAR = 2
FAR = 2
FAR_TOP = 4
MATVECS = 3
BRANCH_LEAVES = 32
NBRANCH = 96
NNODE = 768
NLEAF = 3072
N_SUB = 8


def draw_start_vec(key, part):
    rows = jnp.arange(NLEAF, dtype=jnp.float32) / float(NLEAF)
    amplitude = (1.0 + 0.75 * rows)[:, None]
    values = jnp.clip(jax.random.normal(key, (NLEAF, LEAF), jnp.float32), -6.0, 6.0)
    return values * amplitude


def place_ends(array, stream_key, smallest, largest):
    longest = array.shape.index(max(array.shape))
    spots = []
    for shift in (0, 1):
        where = [jax.random.randint(jax.random.fold_in(stream_key, axis), (), 0, length) for axis, length in enumerate(array.shape)]
        where[longest] = (where[longest] + shift) % array.shape[longest]
        spots.append(tuple(where))
    return array.at[spots[0]].set(smallest).at[spots[1]].set(largest)


def level_of(stream_key, shape, shards, least, high):
    level = 1.0
    for dim, blocks in shards:
        heights = jax.random.uniform(jax.random.fold_in(jax.random.fold_in(stream_key, 6), dim), (blocks,), jnp.float32, least / len(shards), high / len(shards))
        level = level * jnp.repeat(jnp.exp(heights), shape[dim] // blocks).reshape((-1,) + (1,) * (len(shape) - 1 - dim))
    return level


def normal_values(own_key, extent, scale, bound, pieces=(), kind=jnp.bfloat16):
    result = scale * jax.random.normal(own_key, extent, jnp.float32)
    if pieces:
        result = result * level_of(own_key, extent, pieces, -0.22, 0.18)
    return jnp.clip(result, -bound, bound).astype(kind)


def setup_inputs(seed: int = 0) -> dict:
    streams_of = jax.random.split(jax.random.key(seed), 11)
    start_vec = draw_start_vec(jax.random.fold_in(streams_of[10], 71), 0)
    near_blocks = normal_values(streams_of[1], (NLEAF, NEAR, LEAF, LEAF), (NEAR * LEAF) ** -0.5, 0.25, ((0, 768),))
    near_ids = place_ends(jax.random.randint(streams_of[2], (NLEAF, NEAR - 1), 0, 3 * BRANCH_LEAVES), jax.random.fold_in(streams_of[2], 1), 0, (3 * BRANCH_LEAVES) - 1).astype(jnp.int32)
    far_ids = place_ends(jax.random.randint(streams_of[3], (NLEAF, FAR), 0, BRANCH_LEAVES), jax.random.fold_in(streams_of[3], 1), 0, BRANCH_LEAVES - 1).astype(jnp.int32)
    leaf_basis = normal_values(streams_of[4], (NLEAF, RANK, LEAF), LEAF ** -0.5, 0.375, ((0, 768),))
    leaf_coupling = normal_values(streams_of[5], (NLEAF, RANK, FAR * RANK), (FAR * RANK) ** -0.5, 0.5, ((0, 768),))
    node_transfer = normal_values(streams_of[6], (NNODE, RANK, LEAVES_DEV * RANK), (LEAVES_DEV * RANK) ** -0.5, 0.375, ((0, 768),))
    branch_transfer = normal_values(streams_of[7], (NNODE, RANK, RANK), RANK ** -0.5, 0.75, ((0, 768),))
    top_ids = place_ends(jax.random.randint(streams_of[8], (NBRANCH, FAR_TOP), 0, NBRANCH), jax.random.fold_in(streams_of[8], 1), 0, NBRANCH - 1).astype(jnp.int32)
    top_coupling = normal_values(streams_of[9], (NBRANCH, RANK, FAR_TOP * RANK), (FAR_TOP * RANK) ** -0.5, 0.375, ((0, 96),))
    return dict(start_vec=start_vec, near_blocks=near_blocks, near_ids=near_ids, far_ids=far_ids, leaf_basis=leaf_basis, leaf_coupling=leaf_coupling, node_transfer=node_transfer, branch_transfer=branch_transfer, top_ids=top_ids, top_coupling=top_coupling)


def apply_matrix(vector, near_blocks, near_ids, far_ids, leaf_basis, leaf_coupling, node_transfer, branch_transfer, top_ids, top_coupling):
    highest = lax.Precision.HIGHEST
    vec_bf = vector.astype(jnp.bfloat16)
    basis_f = leaf_basis.astype(jnp.float32)
    coef_bf = jnp.einsum('lrk,lk->lr', basis_f, vec_bf.astype(jnp.float32)).astype(jnp.bfloat16)
    node_in = coef_bf.reshape(NNODE, LEAVES_DEV * RANK).astype(jnp.float32)
    transfer_f = node_transfer.astype(jnp.float32)
    node_coef = jnp.einsum('nrk,nk->nr', transfer_f, node_in)
    upper_f = branch_transfer.astype(jnp.float32)
    node_term = jnp.einsum('nrs,ns->nr', upper_f, node_coef, precision=highest).astype(jnp.bfloat16)
    branch_coef = lax.optimization_barrier(jnp.sum(node_term.astype(jnp.float32).reshape(NBRANCH, N_SUB, RANK), axis=1)).astype(jnp.bfloat16)
    partners = branch_coef[top_ids].reshape(NBRANCH, FAR_TOP * RANK).astype(jnp.float32)
    branch_local = jnp.einsum('brk,bk->br', top_coupling.astype(jnp.float32), partners)
    node_branch = jnp.repeat(branch_local, N_SUB, axis=0)
    node_local = jnp.einsum('nrs,nr->ns', upper_f, node_branch, precision=highest)
    leaf_down = jnp.einsum('nrk,nr->nk', transfer_f, node_local, precision=highest).reshape(NLEAF, RANK)
    branch_start = jnp.arange(NLEAF, dtype=jnp.int32) // BRANCH_LEAVES * BRANCH_LEAVES
    far_index = (branch_start[:, None] + far_ids).astype(jnp.int32)
    far_coef = coef_bf[far_index].reshape(NLEAF, FAR * RANK).astype(jnp.float32)
    leaf_far = jnp.einsum('lrk,lk->lr', leaf_coupling.astype(jnp.float32), far_coef)
    local_coef = (leaf_down + leaf_far).astype(jnp.bfloat16)
    far_out = jnp.einsum('lrk,lr->lk', basis_f, local_coef.astype(jnp.float32))
    padded = jnp.pad(vec_bf, ((BRANCH_LEAVES, BRANCH_LEAVES), (0, 0)))
    near_index = (branch_start[:, None] + near_ids).astype(jnp.int32)
    picked = padded[near_index]
    near_input = jnp.concatenate([vec_bf[:, None, :], picked], axis=1)
    blocks_grouped = near_blocks.reshape(NBRANCH, BRANCH_LEAVES, NEAR, LEAF, LEAF)
    input_grouped = near_input.reshape(NBRANCH, BRANCH_LEAVES, NEAR, LEAF)

    def branch_near(pair):
        blocks, inputs = pair
        return jnp.einsum('lsij,lsj->li', blocks.astype(jnp.float32), inputs.astype(jnp.float32))
    near_out = lax.map(branch_near, (blocks_grouped, input_grouped)).reshape(NLEAF, LEAF)
    return 0.5 * vector + near_out + far_out

def reference(start_vec, near_blocks, near_ids, far_ids, leaf_basis, leaf_coupling, node_transfer, branch_transfer, top_ids, top_coupling):
    total = float(NLEAF * LEAF)
    first = start_vec * lax.rsqrt(jnp.sum(start_vec * start_vec) / total + 1e-06)
    vectors = [first]
    hessen = jnp.zeros((MATVECS + 1, MATVECS), jnp.float32)
    for column in range(MATVECS):
        image = apply_matrix(vectors[column], near_blocks, near_ids, far_ids, leaf_basis, leaf_coupling, node_transfer, branch_transfer, top_ids, top_coupling)
        dots = jnp.stack([jnp.sum(earlier * image) for earlier in vectors]) / total
        square = jnp.sum(image * image) / total
        remain = square - jnp.sum(dots * dots)
        scale = jnp.sqrt(jnp.maximum(remain, 0.01 * square))
        update = image
        for index_i in range(column + 1):
            update = update - dots[index_i] * vectors[index_i]
        vectors.append(update / scale)
        hessen = hessen.at[:column + 1, column].set(dots)
        hessen = hessen.at[column + 1, column].set(scale)
    return (jnp.stack(vectors), hessen)
```

```python
import functools

import jax
import jax.numpy as jnp
from jax import lax
from jax.experimental import pallas as pl
from jax.experimental.pallas import tpu as pltpu
from jax.sharding import PartitionSpec as P

MESH = pl.DeviceIdType.MESH
F32 = jnp.float32
BF16 = jnp.bfloat16
STEPS = 3
RING = 8


def dot_nt(a, b):
    return lax.dot_general(a, b, (((1,), (1,)), ((), ())), preferred_element_type=F32)


def dot_nn(a, b):
    return lax.dot_general(a, b, (((1,), (0,)), ((), ())), preferred_element_type=F32)


def split(x):
    high = x.astype(BF16).astype(F32)
    return jnp.concatenate([high, x - high], axis=0).astype(BF16)


def outward(j, n):
    half = (j + 1) // 2
    return n // 2 + half - 2 * half * (j % 2)


def kernel(
    nl,
    ns,
    ny,
    near_ids,
    far_ids,
    top_ids,
    start_h,
    near_h,
    lb_h,
    lc_h,
    nt_h,
    bt_h,
    tc_h,
    basis_ref,
    hess_ref,
    start_v,
    near_v,
    lb_v,
    lc_v,
    nt_v,
    bt_v,
    tc_v,
    t_v,
    r1_0,
    r1_1,
    r1_2,
    r1_3,
    r2_0,
    r2_1,
    r2_2,
    r2_3,
    x_0,
    x_1,
    x_2,
    c_0,
    c_1,
    c_2,
    in_sem,
    r1_send,
    r1_recv,
    r2_send,
    r2_recv,
    x_send,
    x_recv,
    c_send,
    c_recv,
):
    leaf, sub = lax.axis_index("leaf"), lax.axis_index("sub")
    r1, r2 = (r1_0, r1_1, r1_2, r1_3), (r2_0, r2_1, r2_2, r2_3)
    xall, call = (x_0, x_1, x_2), (c_0, c_1, c_2)
    nz = nl // ny
    z, y = leaf // ny, leaf % ny
    pairs = (
        (start_h, start_v),
        (bt_h, bt_v),
        (nt_h, nt_v),
        (lb_h, lb_v),
        (tc_h, tc_v),
        (lc_h, lc_v),
        (near_h, near_v),
    )
    loads = [pltpu.make_async_copy(s, d, in_sem.at[i]) for i, (s, d) in enumerate(pairs)]
    for load in loads:
        load.start()

    def branch_at(j):
        dz, dy = outward(j // ny, nz), outward(j % ny, ny)
        return lax.rem(z + dz, nz) * ny + lax.rem(y + dy, ny)

    barrier = pltpu.get_barrier_semaphore()

    def greet_branch(j, c):
        pl.semaphore_signal(
            barrier, inc=1, device_id=(branch_at(j), sub), device_id_type=MESH
        )
        return c

    def halo_at(j):
        side = j // ns
        back = 3 * (side // 2)
        to = lax.rem(leaf + side - back + nl, nl)
        return to, lax.rem(sub + j, ns), 1 - side + back

    def greet_halo(j, c):
        to, other, _ = halo_at(j)
        pl.semaphore_signal(barrier, inc=1, device_id=(to, other), device_id_type=MESH)
        return c

    lax.fori_loop(1, 3 * ns, greet_halo, 0)
    lax.fori_loop(0, nl - 1, greet_branch, 0)

    row4 = lax.broadcasted_iota(jnp.int32, (4, 256), 0)
    row8 = lax.broadcasted_iota(jnp.int32, (8, 256), 0)
    lane = lax.broadcasted_iota(jnp.int32, (1, 128), 1)
    total = float(nl * ns * 4 * 256)

    for load in loads[:4]:
        load.wait()
    up = dot_nn(bt_v[0], nt_v[0]).astype(BF16)
    for leaf_i in range(4):
        t_v[:, 256 * leaf_i : 256 * (leaf_i + 1)] = dot_nn(
            up[:, 64 * leaf_i : 64 * (leaf_i + 1)], lb_v[leaf_i]
        ).astype(BF16)

    def fold(p):
        s = jnp.sum(p, axis=0, keepdims=True) * (1.0 / total)
        s = s[:, :128] + s[:, 128:]
        return s + pltpu.roll(s, 64, 1)

    def term_of(x8):
        x8f = x8.astype(F32)
        parts = [jnp.where(row8 % 4 == i, x8f, 0.0).astype(BF16) for i in range(4)]
        out = dot_nt(jnp.concatenate(parts, axis=1), t_v[...])
        return jnp.sum(out, axis=0, keepdims=True)

    def send_r1(k):
        def go(j, c):
            pltpu.make_async_remote_copy(
                r1[k].at[sub],
                r1[k].at[sub],
                r1_send.at[k],
                r1_recv.at[k],
                device_id=(leaf, lax.rem(sub + j, ns)),
                device_id_type=MESH,
            ).start()
            return c

        lax.fori_loop(1, ns, go, 0)

    def bytes_wait(ref, sem):
        pltpu.make_async_copy(ref, ref, sem).wait()

    def send_r2(k):
        def go(j, c):
            pltpu.make_async_remote_copy(
                r2[k].at[leaf],
                r2[k].at[leaf],
                r2_send.at[k],
                r2_recv.at[k],
                device_id=(branch_at(j), sub),
                device_id_type=MESH,
            ).start()
            return c

        lax.fori_loop(0, nl - 1, go, 0)

    def sum_r1(k):
        bytes_wait(r1[k].at[pl.ds(0, ns - 1)], r1_recv.at[k])
        for row in range(2):
            acc = r1[k][0, row]
            for j in range(1, ns):
                acc = acc + r1[k][j, row]
            r2[k][leaf, row] = acc

    def send_x(k):
        def go(j, c):
            to, other, slot = halo_at(j)
            pltpu.make_async_remote_copy(
                xall[k].at[ns + sub],
                xall[k].at[slot * ns + sub],
                x_send.at[k],
                x_recv.at[k],
                device_id=(to, other),
                device_id_type=MESH,
            ).start()
            return c

        lax.fori_loop(1, 3 * ns, go, 0)

    def send_c(k):
        def go(j, c):
            pltpu.make_async_remote_copy(
                call[k].at[sub],
                call[k].at[sub],
                c_send.at[k],
                c_recv.at[k],
                device_id=(leaf, lax.rem(sub + j, ns)),
                device_id_type=MESH,
            ).start()
            return c

        lax.fori_loop(1, ns, go, 0)

    def store_coef(k, x8):
        out = dot_nt(x8, lb_v[...].reshape(256, 256))
        out = out[:4] + out[4:]
        for i in range(4):
            piece = out[i : i + 1, 128 * (i // 2) : 128 * (i // 2) + 128]
            piece = jnp.where((lane // 64) == i % 2, piece, 0.0)
            call[k][sub, i] = piece + pltpu.roll(piece, 64, 1)

    def local_part(k, x8):
        bytes_wait(xall[k].at[pl.ds(0, 3 * ns - 1)], x_recv.at[k])
        bytes_wait(call[k].at[pl.ds(0, ns - 1)], c_recv.at[k])
        near_rows, far_rows = [], []
        for i in range(4):
            one = near_ids[i, 0]
            outside = jnp.logical_or(
                jnp.logical_and(leaf == 0, one < 4 * ns),
                jnp.logical_and(leaf == nl - 1, one >= 8 * ns),
            )
            keep = jnp.where(outside, 0.0, 1.0)
            near_rows.append(xall[k][one // 4, one % 4] * keep)
            first, second = far_ids[i, 0], far_ids[i, 1]
            far_rows.append(
                jnp.where(
                    lane < 64,
                    call[k][first // 4, first % 4],
                    call[k][second // 4, second % 4],
                )
            )
        p8 = split(jnp.concatenate(near_rows, axis=0))
        f8 = split(jnp.concatenate(far_rows, axis=0))
        out = jnp.zeros((4, 256), F32)
        for i in range(4):
            o8 = dot_nt(x8, near_v[i, 0]) + dot_nt(p8, near_v[i, 1])
            g8 = dot_nt(f8, lc_v[i])
            o4 = o8[:4] + o8[4:] + dot_nn((g8[:4] + g8[4:]).astype(BF16), lb_v[i])
            out = jnp.where(row4 == i, o4, out)
        return out

    def dots_total(k, row):
        acc = jnp.zeros((1, 128), F32)
        for c in range(0, nl, min(nl, 8)):
            acc = acc + jnp.sum(r2[k][pl.ds(c, min(nl, 8)), row], axis=0)
        return acc

    def half_sum(v, half):
        return jnp.sum(jnp.where((lane // 64) == half, v, 0.0), axis=1, keepdims=True)

    us = [start_v[...]]
    gram = {}
    nus = []
    halves = [None, None]
    for k in range(STEPS):
        x = us[k]
        x8 = split(x)
        term = term_of(x8)
        term = jnp.concatenate([term, term], axis=1)
        r1[k][sub, 0] = jnp.where(lane < 64, term, fold(x * x))
        if k == 0:
            r1[k][sub, 1] = jnp.zeros((1, 128), F32)
        else:
            r1[k][sub, 1] = jnp.where(lane < 64, fold(x * us[0]), fold(x * us[(k == 2) * 1]))
        if k == 0:
            pl.semaphore_wait(barrier, nl - 1 + 3 * ns - 1)
        send_r1(k)
        for i in range(4):
            xall[k][ns + sub, i] = x[i : i + 1]
        send_x(k)
        store_coef(k, x8)
        send_c(k)
        sum_r1(k)
        bytes_wait(xall[k].at[pl.ds(0, 3 * ns - 1)], x_send.at[k])
        bytes_wait(call[k].at[pl.ds(0, ns - 1)], c_send.at[k])
        send_r2(k)
        if k == 0:
            for load in loads[4:]:
                load.wait()
        local = local_part(k, x8)
        bytes_wait(r2[k].at[pl.ds(0, nl - 1)], r2_recv.at[k])
        picked = [r2[k][top_ids[0, s], 0] for s in range(4)]
        pair0 = jnp.where(lane < 64, picked[0], pltpu.roll(picked[1], 64, 1))
        pair1 = jnp.where(lane < 64, picked[2], pltpu.roll(picked[3], 64, 1))
        chosen = split(jnp.concatenate([pair0, pair1], axis=1))
        branchl = jnp.sum(dot_nt(chosen, tc_v[0]), axis=0, keepdims=True)
        down = jnp.sum(dot_nn(split(branchl), t_v[...]), axis=0, keepdims=True)
        down = jnp.concatenate([down[:, 256 * i : 256 * (i + 1)] for i in range(4)], axis=0)
        sums = dots_total(k, 0)
        gram[k, k] = half_sum(sums, 1)
        if k >= 1:
            sums = dots_total(k, 1)
            gram[k, 0] = half_sum(sums, 0)
            if k == 2:
                gram[k, 1] = half_sum(sums, 1)
        guarded = jnp.maximum(gram[k, k], 1e-30)
        nus.append(jnp.sqrt(guarded))
        us.append((local + down) * lax.rsqrt(guarded))

    x = us[3]
    r1[3][sub, 0] = jnp.where(lane < 64, fold(x * us[2]), fold(x * x))
    r1[3][sub, 1] = jnp.where(lane < 64, fold(x * us[0]), fold(x * us[1]))
    send_r1(3)

    def g(i, j):
        return gram[max(i, j), min(i, j)]

    zero = jnp.zeros((1, 1), F32)
    coefs = [[lax.rsqrt(gram[0, 0] + 1e-06)]]
    basis_ref[0] = us[0] * coefs[0][0]
    hess = {}

    def column(j):
        a = coefs[j]
        w = []
        for i in range(j + 2):
            v = zero
            if i <= j:
                v = v + 0.5 * a[i]
            if i >= 1:
                v = v + nus[i - 1] * a[i - 1]
            w.append(v)
        gw = [sum((g(i, m) * w[m] for m in range(1, j + 2)), g(i, 0) * w[0]) for i in range(j + 2)]
        square = sum((w[i] * gw[i] for i in range(1, j + 2)), w[0] * gw[0])
        remain = square
        new = list(w)
        for i in range(j + 1):
            h = sum((coefs[i][m] * gw[m] for m in range(1, i + 1)), coefs[i][0] * gw[0])
            hess[i, j] = h
            remain = remain - h * h
            for m in range(i + 1):
                new[m] = new[m] - h * coefs[i][m]
        scale = jnp.sqrt(jnp.maximum(remain, 0.01 * square))
        hess[j + 1, j] = scale
        inverse = 1.0 / scale
        coefs.append([v * inverse for v in new])

    def store_basis(j):
        acc = us[0] * coefs[j][0]
        for m in range(1, j + 1):
            acc = acc + us[m] * coefs[j][m]
        basis_ref[j] = acc

    column(0)
    column(1)
    store_basis(1)
    store_basis(2)
    sum_r1(3)
    send_r2(3)
    bytes_wait(r2[3].at[pl.ds(0, nl - 1)], r2_recv.at[3])
    sums = dots_total(3, 0)
    gram[3, 2], gram[3, 3] = half_sum(sums, 0), half_sum(sums, 1)
    sums = dots_total(3, 1)
    gram[3, 0], gram[3, 1] = half_sum(sums, 0), half_sum(sums, 1)
    column(2)
    store_basis(3)
    rows = lax.broadcasted_iota(jnp.int32, (4, 3), 0)
    cols = lax.broadcasted_iota(jnp.int32, (4, 3), 1)
    table = jnp.zeros((4, 3), F32)
    for (i, j), h in hess.items():
        table = jnp.where(jnp.logical_and(rows == i, cols == j), h, table)
    hess_ref[...] = table

    for k in range(4):
        bytes_wait(r1[k].at[pl.ds(0, ns - 1)], r1_send.at[k])
        bytes_wait(r2[k].at[pl.ds(0, nl - 1)], r2_send.at[k])


def solution(mesh):
    nl, ns = mesh.shape["leaf"], mesh.shape["sub"]
    ny = RING if nl % RING == 0 else 1

    def per_device(
        start_vec,
        near_blocks,
        near_ids,
        far_ids,
        leaf_basis,
        leaf_coupling,
        node_transfer,
        branch_transfer,
        top_ids,
        top_coupling,
    ):
        smem = pl.BlockSpec(memory_space=pltpu.SMEM)
        hbm = pl.BlockSpec(memory_space=pl.ANY)
        vmem = pl.BlockSpec(memory_space=pltpu.VMEM)
        dma = pltpu.SemaphoreType.DMA
        return pl.pallas_call(
            functools.partial(kernel, nl, ns, ny),
            out_shape=(
                jax.ShapeDtypeStruct((4, 4, 256), F32),
                jax.ShapeDtypeStruct((4, 3), F32),
            ),
            in_specs=[smem] * 3 + [hbm] * 7,
            out_specs=(vmem, vmem),
            scratch_shapes=[
                pltpu.VMEM((4, 256), F32),
                pltpu.VMEM((4, 2, 256, 256), BF16),
                pltpu.VMEM((4, 64, 256), BF16),
                pltpu.VMEM((4, 64, 128), BF16),
                pltpu.VMEM((1, 64, 256), BF16),
                pltpu.VMEM((1, 64, 64), BF16),
                pltpu.VMEM((1, 64, 256), BF16),
                pltpu.VMEM((64, 1024), BF16),
                *[pltpu.VMEM((ns, 2, 1, 128), F32)] * 4,
                *[pltpu.VMEM((nl, 2, 1, 128), F32)] * 4,
                *[pltpu.VMEM((3 * ns, 4, 1, 256), F32)] * 3,
                *[pltpu.VMEM((ns, 4, 1, 128), F32)] * 3,
                dma((7,)),
                dma((4,)),
                dma((4,)),
                dma((4,)),
                dma((4,)),
                dma((3,)),
                dma((3,)),
                dma((3,)),
                dma((3,)),
            ],
            compiler_params=pltpu.CompilerParams(
                collective_id=0, has_side_effects=True, vmem_limit_bytes=40 * 2**20
            ),
        )(
            near_ids,
            far_ids,
            top_ids,
            start_vec,
            near_blocks,
            leaf_basis,
            leaf_coupling,
            node_transfer,
            branch_transfer,
            top_coupling,
        )

    placed = (
        P(("leaf", "sub"), None),
        P(("leaf", "sub"), None, None, None),
        P(("leaf", "sub"), None),
        P(("leaf", "sub"), None),
        P(("leaf", "sub"), None, None),
        P(("leaf", "sub"), None, None),
        P(("leaf", "sub"), None, None),
        P(("leaf", "sub"), None, None),
        P("leaf", None),
        P("leaf", None, None),
    )
    return jax.shard_map(
        per_device,
        mesh=mesh,
        in_specs=placed,
        out_specs=(P(None, ("leaf", "sub"), None), P()),
        check_vma=False,
    )
```

```python
import functools

import jax
import jax.numpy as jnp
from jax import lax
from jax.experimental import pallas as pl
from jax.experimental.pallas import tpu as pltpu
from jax.sharding import PartitionSpec as P

MESH = pl.DeviceIdType.MESH
F32 = jnp.float32
BF16 = jnp.bfloat16
STEPS = 3
RING = 8


def dot_nt(a, b):
    return lax.dot_general(a, b, (((1,), (1,)), ((), ())), preferred_element_type=F32)


def dot_nn(a, b):
    return lax.dot_general(a, b, (((1,), (0,)), ((), ())), preferred_element_type=F32)


def split(x):
    high = x.astype(BF16).astype(F32)
    return jnp.concatenate([high, x - high], axis=0).astype(BF16)


def outward(j, n):
    half = (j + 1) // 2
    return n // 2 + half - 2 * half * (j % 2)


def kernel(
    nl,
    ns,
    ny,
    near_ids_h,
    far_ids_h,
    top_ids_h,
    start_h,
    near_h,
    lb_h,
    lc_h,
    nt_h,
    bt_h,
    tc_h,
    basis_ref,
    hess_ref,
    near_ids,
    far_ids,
    top_ids,
    start_v,
    near_v,
    lb_v,
    lc_v,
    nt_v,
    bt_v,
    tc_v,
    t_v,
    tcw_v,
    gram_v,
    r1_0,
    r1_1,
    r1_2,
    r1_3,
    r2_0,
    r2_1,
    r2_2,
    r2_3,
    x_0,
    x_1,
    x_2,
    c_0,
    c_1,
    c_2,
    in_sem,
    r1_send,
    r1_recv,
    r2_send,
    r2_recv,
    x_send,
    x_recv,
    c_send,
    c_recv,
    g_send,
    g_recv,
):
    leaf, sub = lax.axis_index("leaf"), lax.axis_index("sub")
    r1, r2 = (r1_0, r1_1, r1_2, r1_3), (r2_0, r2_1, r2_2, r2_3)
    xall, call = (x_0, x_1, x_2), (c_0, c_1, c_2)
    nz = nl // ny
    z, y = leaf // ny, leaf % ny
    pairs = (
        (start_h, start_v),
        (bt_h, bt_v),
        (nt_h, nt_v),
        (lb_h, lb_v),
        (tc_h, tc_v),
        (lc_h, lc_v),
        (near_h, near_v),
        (near_ids_h, near_ids),
        (far_ids_h, far_ids),
        (top_ids_h, top_ids),
    )
    loads = [pltpu.make_async_copy(s, d, in_sem.at[i]) for i, (s, d) in enumerate(pairs)]
    for load in loads:
        load.start()

    columns = [lax.rem(y + outward(j, ny), ny) for j in range(ny)]

    def each_branch(act):
        def ring(j, c):
            row = lax.rem(z + outward(j, nz), nz) * ny
            for column in columns:
                act(row + column)
            return c

        lax.fori_loop(0, nz - 1, ring, 0)
        for column in columns[:-1]:
            act(z * ny + column)

    barrier = pltpu.get_barrier_semaphore()

    def greet_branch(to):
        pl.semaphore_signal(barrier, inc=1, device_id=(to, sub), device_id_type=MESH)

    def halo_at(j):
        side = j // ns
        back = 3 * (side // 2)
        to = lax.rem(leaf + side - back + nl, nl)
        return to, lax.rem(sub + j, ns), 1 - side + back

    def greet_halo(j, c):
        to, other, _ = halo_at(j)
        pl.semaphore_signal(barrier, inc=1, device_id=(to, other), device_id_type=MESH)
        return c

    each_branch(greet_branch)
    lax.fori_loop(1, 3 * ns, greet_halo, 0)

    row4 = lax.broadcasted_iota(jnp.int32, (4, 256), 0)
    row8 = lax.broadcasted_iota(jnp.int32, (8, 256), 0)
    lane = lax.broadcasted_iota(jnp.int32, (1, 128), 1)
    total = float(nl * ns * 4 * 256)

    for load in loads[:4]:
        load.wait()
    up = dot_nn(bt_v[0], nt_v[0]).astype(BF16)
    for leaf_i in range(4):
        t_v[:, 256 * leaf_i : 256 * (leaf_i + 1)] = dot_nn(
            up[:, 64 * leaf_i : 64 * (leaf_i + 1)], lb_v[leaf_i]
        ).astype(BF16)

    def fold(p):
        s = jnp.sum(p, axis=0, keepdims=True) * (1.0 / total)
        s = s[:, :128] + s[:, 128:]
        return s + pltpu.roll(s, 64, 1)

    def term_of(x8):
        x8f = x8.astype(F32)
        parts = [jnp.where(row8 % 4 == i, x8f, 0.0).astype(BF16) for i in range(4)]
        out = dot_nt(jnp.concatenate(parts, axis=1), t_v[...])
        out = jnp.sum(out, axis=0, keepdims=True)
        return jnp.concatenate([out, out], axis=1)

    def send_r1(k):
        def go(j, c):
            pltpu.make_async_remote_copy(
                r1[k].at[sub],
                r1[k].at[sub],
                r1_send.at[k],
                r1_recv.at[k],
                device_id=(leaf, lax.rem(sub + j, ns)),
                device_id_type=MESH,
            ).start()
            return c

        lax.fori_loop(1, ns, go, 0)

    def bytes_wait(ref, sem):
        pltpu.make_async_copy(ref, ref, sem).wait()

    def send_r2(k):
        def go(to):
            pltpu.make_async_remote_copy(
                r2[k].at[leaf],
                r2[k].at[leaf],
                r2_send.at[k],
                r2_recv.at[k],
                device_id=(to, sub),
                device_id_type=MESH,
            ).start()

        each_branch(go)

    def branch_sum(k):
        bytes_wait(r1[k].at[pl.ds(0, ns - 1)], r1_recv.at[k])
        sums = []
        for row in range(3):
            acc = r1[k][0, row]
            for j in range(1, ns):
                acc = acc + r1[k][j, row]
            sums.append(acc)
        return sums

    def send_gram():
        def go(j, c):
            pltpu.make_async_remote_copy(
                gram_v.at[sub],
                gram_v.at[sub],
                g_send,
                g_recv,
                device_id=(leaf, lax.rem(sub + j, ns)),
                device_id_type=MESH,
            ).start()
            return c

        lax.fori_loop(1, ns, go, 0)

    def send_x(k):
        def go(j, c):
            to, other, slot = halo_at(j)
            pltpu.make_async_remote_copy(
                xall[k].at[ns + sub],
                xall[k].at[slot * ns + sub],
                x_send.at[k],
                x_recv.at[k],
                device_id=(to, other),
                device_id_type=MESH,
            ).start()
            return c

        lax.fori_loop(1, 3 * ns, go, 0)

    def send_c(k):
        def go(j, c):
            pltpu.make_async_remote_copy(
                call[k].at[sub],
                call[k].at[sub],
                c_send.at[k],
                c_recv.at[k],
                device_id=(leaf, lax.rem(sub + j, ns)),
                device_id_type=MESH,
            ).start()
            return c

        lax.fori_loop(1, ns, go, 0)

    def store_coef(k, x8):
        out = dot_nt(x8, lb_v[...].reshape(256, 256))
        out = out[:4] + out[4:]
        for i in range(4):
            piece = out[i : i + 1, 128 * (i // 2) : 128 * (i // 2) + 128]
            piece = jnp.where((lane // 64) == i % 2, piece, 0.0)
            call[k][sub, i] = piece + pltpu.roll(piece, 64, 1)

    def own_part(x8):
        out = jnp.zeros((4, 256), F32)
        for i in range(4):
            o8 = dot_nt(x8, near_v[i, 0])
            out = jnp.where(row4 == i, o8[:4] + o8[4:], out)
        return out

    def partner_part(k):
        bytes_wait(xall[k].at[pl.ds(0, 3 * ns - 1)], x_recv.at[k])
        bytes_wait(call[k].at[pl.ds(0, ns - 1)], c_recv.at[k])
        near_rows, far_rows = [], []
        for i in range(4):
            one = near_ids[0, i]
            outside = jnp.logical_or(
                jnp.logical_and(leaf == 0, one < 4 * ns),
                jnp.logical_and(leaf == nl - 1, one >= 8 * ns),
            )
            keep = jnp.where(outside, 0.0, 1.0)
            near_rows.append(xall[k][one // 4, one % 4] * keep)
            first, second = far_ids[0, i], far_ids[1, i]
            far_rows.append(
                jnp.where(
                    lane < 64,
                    call[k][first // 4, first % 4],
                    call[k][second // 4, second % 4],
                )
            )
        p8 = split(jnp.concatenate(near_rows, axis=0))
        f8 = split(jnp.concatenate(far_rows, axis=0))
        out = jnp.zeros((4, 256), F32)
        for i in range(4):
            o8 = dot_nt(p8, near_v[i, 1])
            g8 = dot_nt(f8, lc_v[i])
            o4 = o8[:4] + o8[4:] + dot_nn((g8[:4] + g8[4:]).astype(BF16), lb_v[i])
            out = jnp.where(row4 == i, o4, out)
        return out

    def over_table(k, op):
        step = min(nl, 8)
        acc = None
        for c in range(0, nl, step):
            rows = r2[k][pl.ds(c, step)]
            part = jnp.max(jnp.abs(rows), axis=0) if op == "max" else jnp.sum(rows, axis=0)
            if acc is not None:
                part = jnp.maximum(acc, part) if op == "max" else acc + part
            acc = part
        return acc

    def half_sum(v, half):
        return jnp.sum(jnp.where((lane // 64) == half, v, 0.0), axis=1, keepdims=True)

    def exchange_leaves(k, x, x8):
        for i in range(4):
            xall[k][ns + sub, i] = x[i : i + 1]
        send_x(k)
        store_coef(k, x8)
        send_c(k)

    def leaves_sent(k):
        bytes_wait(xall[k].at[pl.ds(0, 3 * ns - 1)], x_send.at[k])
        bytes_wait(call[k].at[pl.ds(0, ns - 1)], c_send.at[k])

    low = lane < 64
    us = [start_v[...]]
    x8 = split(us[0])
    r1[0][sub, 0] = term_of(x8)
    r1[0][sub, 1] = fold(us[0] * us[0])
    r1[0][sub, 2] = jnp.zeros((1, 128), F32)
    pl.semaphore_wait(barrier, nl - 1 + 3 * ns - 1)
    send_r1(0)
    exchange_leaves(0, us[0], x8)
    both = dot_nt(t_v[...], t_v[...])
    gram_v[sub] = jnp.concatenate([both, both], axis=1)
    order = [(i, j) for i in range(4) for j in range(i + 1)]
    pending = jnp.zeros((1, 128), F32)

    def put(row, i, j, value):
        return row + jnp.where(lane == order.index((i, j)), value, 0.0)

    sums = branch_sum(0)
    r2[0][leaf] = sums[0]
    send_r2(0)
    send_gram()
    pending = put(pending, 0, 0, half_sum(sums[1], 0))
    branchc = [sums[0]]
    for load in loads[4:]:
        load.wait()
    before = jnp.ones((1, 1), F32)
    nus = []
    own = own_part(x8)
    for k in range(STEPS):
        local = own + partner_part(k)
        r1[k + 1][sub, 0] = term_of(split(local))
        dots = [fold(local * u) for u in us]
        r1[k + 1][sub, 1] = jnp.where(low, fold(local * local), dots[0])
        r1[k + 1][sub, 2] = jnp.where(low, dots[min(k, 1)], dots[k])
        send_r1(k + 1)
        if k == 0:
            bytes_wait(gram_v.at[pl.ds(0, ns - 1)], g_recv)
            whole = gram_v[0]
            for j in range(1, ns):
                whole = whole + gram_v[j]
            both = dot_nn(whole[:, :64].astype(BF16), tc_v[0]).astype(BF16)
            tcw_v[:64] = both
            tcw_v[64:128] = both
            tcw_v[128:192] = tc_v[0]
            tcw_v[192:] = tc_v[0]
        sums = branch_sum(k + 1)
        bytes_wait(r2[k].at[pl.ds(0, nl - 1)], r2_recv.at[k])
        picked = [r2[k][top_ids[0, s]] for s in range(4)]
        pair0 = jnp.where(low, picked[0], picked[1])
        pair1 = jnp.where(low, picked[2], picked[3])
        chosen = split(jnp.concatenate([pair0, pair1], axis=1))
        got = dot_nt(chosen, tcw_v[...])
        got = (got[:1] + got[1:]) * before
        added, branchl = got[:, :128], got[:, 128:]
        if k < 2:
            later = sums[0] + added
            r2[k + 1][leaf] = later
            send_r2(k + 1)
            biggest = jnp.max(over_table(k, "max"), axis=1, keepdims=True) * before
            alpha = 1.0 / jnp.maximum(biggest, 1.0)
        else:
            alpha = jnp.full((1, 1), 2.0**-20, F32)
        nus.append(1.0 / alpha)
        scaled = branchl * (alpha * (1.0 / total))
        factors = jnp.where(low, alpha * (2.0 * sums[0] + added), branchc[0])
        first = sums[1] * jnp.where(low, alpha * alpha, alpha) + scaled * factors
        pending = put(pending, k + 1, k + 1, half_sum(first, 0))
        pending = put(pending, k + 1, 0, half_sum(first, 1))
        if k >= 1:
            second = sums[2] * alpha + scaled * jnp.where(low, branchc[1], branchc[k])
            pending = put(pending, k + 1, 1, half_sum(second, 0))
            if k == 2:
                pending = put(pending, 3, 2, half_sum(second, 1))
        if k == 2:
            r2[3][leaf] = pending
            send_r2(3)
        down = jnp.sum(dot_nn(split(branchl[:, :64]), t_v[...]), axis=0, keepdims=True)
        down = jnp.concatenate([down[:, 256 * i : 256 * (i + 1)] for i in range(4)], axis=0)
        x = (local + down) * alpha
        us.append(x)
        if k < 2:
            x8 = split(x)
            exchange_leaves(k + 1, x, x8)
            branchc.append(later * alpha)
            before = alpha
            own = own_part(x8)

    bytes_wait(r2[3].at[pl.ds(0, nl - 1)], r2_recv.at[3])
    sums = over_table(3, "sum")
    gram = {ij: sums[:, i : i + 1] for i, ij in enumerate(order)}

    def g(i, j):
        return gram[max(i, j), min(i, j)]

    zero = jnp.zeros((1, 1), F32)
    coefs = [[lax.rsqrt(gram[0, 0] + 1e-06)]]
    basis_ref[0] = us[0] * coefs[0][0]
    hess = {}

    def column(j):
        a = coefs[j]
        w = []
        for i in range(j + 2):
            v = zero
            if i <= j:
                v = v + 0.5 * a[i]
            if i >= 1:
                v = v + nus[i - 1] * a[i - 1]
            w.append(v)
        gw = [sum((g(i, m) * w[m] for m in range(1, j + 2)), g(i, 0) * w[0]) for i in range(j + 2)]
        square = sum((w[i] * gw[i] for i in range(1, j + 2)), w[0] * gw[0])
        remain = square
        new = list(w)
        for i in range(j + 1):
            h = sum((coefs[i][m] * gw[m] for m in range(1, i + 1)), coefs[i][0] * gw[0])
            hess[i, j] = h
            remain = remain - h * h
            for m in range(i + 1):
                new[m] = new[m] - h * coefs[i][m]
        scale = jnp.sqrt(jnp.maximum(remain, 0.01 * square))
        hess[j + 1, j] = scale
        inverse = 1.0 / scale
        coefs.append([v * inverse for v in new])

    def store_basis(j):
        acc = us[0] * coefs[j][0]
        for m in range(1, j + 1):
            acc = acc + us[m] * coefs[j][m]
        basis_ref[j] = acc

    for j in range(STEPS):
        column(j)
        store_basis(j + 1)
    rows = lax.broadcasted_iota(jnp.int32, (4, 3), 0)
    cols = lax.broadcasted_iota(jnp.int32, (4, 3), 1)
    table = jnp.zeros((4, 3), F32)
    for (i, j), h in hess.items():
        table = jnp.where(jnp.logical_and(rows == i, cols == j), h, table)
    hess_ref[...] = table

    for k in range(4):
        bytes_wait(r1[k].at[pl.ds(0, ns - 1)], r1_send.at[k])
        bytes_wait(r2[k].at[pl.ds(0, nl - 1)], r2_send.at[k])
    for k in range(STEPS):
        leaves_sent(k)
    bytes_wait(gram_v.at[pl.ds(0, ns - 1)], g_send)


def solution(mesh):
    nl, ns = mesh.shape["leaf"], mesh.shape["sub"]
    ny = RING if nl % RING == 0 else 1

    def per_device(
        start_vec,
        near_blocks,
        near_ids,
        far_ids,
        leaf_basis,
        leaf_coupling,
        node_transfer,
        branch_transfer,
        top_ids,
        top_coupling,
    ):
        hbm = pl.BlockSpec(memory_space=pltpu.HBM)
        vmem = pl.BlockSpec(memory_space=pltpu.VMEM)
        dma = pltpu.SemaphoreType.DMA
        return pl.pallas_call(
            functools.partial(kernel, nl, ns, ny),
            out_shape=(
                jax.ShapeDtypeStruct((4, 4, 256), F32),
                jax.ShapeDtypeStruct((4, 3), F32),
            ),
            in_specs=[hbm] * 10,
            out_specs=(vmem, vmem),
            scratch_shapes=[
                pltpu.SMEM((1, 4), jnp.int32),
                pltpu.SMEM((2, 4), jnp.int32),
                pltpu.SMEM((1, 4), jnp.int32),
                pltpu.VMEM((4, 256), F32),
                pltpu.VMEM((4, 2, 256, 256), BF16),
                pltpu.VMEM((4, 64, 256), BF16),
                pltpu.VMEM((4, 64, 128), BF16),
                pltpu.VMEM((1, 64, 256), BF16),
                pltpu.VMEM((1, 64, 64), BF16),
                pltpu.VMEM((1, 64, 256), BF16),
                pltpu.VMEM((64, 1024), BF16),
                pltpu.VMEM((256, 256), BF16),
                pltpu.VMEM((ns, 64, 128), F32),
                *[pltpu.VMEM((ns, 3, 1, 128), F32)] * 4,
                *[pltpu.VMEM((nl, 1, 128), F32)] * 4,
                *[pltpu.VMEM((3 * ns, 4, 1, 256), F32)] * 3,
                *[pltpu.VMEM((ns, 4, 1, 128), F32)] * 3,
                dma((10,)),
                dma((4,)),
                dma((4,)),
                dma((4,)),
                dma((4,)),
                dma((3,)),
                dma((3,)),
                dma((3,)),
                dma((3,)),
                dma,
                dma,
            ],
            compiler_params=pltpu.CompilerParams(
                collective_id=0, has_side_effects=True, vmem_limit_bytes=40 * 2**20
            ),
        )(
            *(
                pltpu.with_memory_space_constraint(v, pltpu.HBM)
                for v in (
                    near_ids.T,
                    far_ids.T,
                    top_ids,
                    start_vec,
                    near_blocks,
                    leaf_basis,
                    leaf_coupling,
                    node_transfer,
                    branch_transfer,
                    top_coupling,
                )
            )
        )

    placed = (
        P(("leaf", "sub"), None),
        P(("leaf", "sub"), None, None, None),
        P(("leaf", "sub"), None),
        P(("leaf", "sub"), None),
        P(("leaf", "sub"), None, None),
        P(("leaf", "sub"), None, None),
        P(("leaf", "sub"), None, None),
        P(("leaf", "sub"), None, None),
        P("leaf", None),
        P("leaf", None, None),
    )
    return jax.shard_map(
        per_device,
        mesh=mesh,
        in_specs=placed,
        out_specs=(P(None, ("leaf", "sub"), None), P()),
        check_vma=False,
    )
```

```python
import functools

import jax
import jax.numpy as jnp
from jax import lax
from jax.experimental import pallas as pl
from jax.experimental.pallas import tpu as pltpu
from jax.sharding import PartitionSpec as P

MESH = pl.DeviceIdType.MESH
F32 = jnp.float32
BF16 = jnp.bfloat16
STEPS = 3
RING = 8


def dot_nt(a, b):
    return lax.dot_general(a, b, (((1,), (1,)), ((), ())), preferred_element_type=F32)


def dot_nn(a, b):
    return lax.dot_general(a, b, (((1,), (0,)), ((), ())), preferred_element_type=F32)


def split(x):
    high = x.astype(BF16).astype(F32)
    return jnp.concatenate([high, x - high], axis=0).astype(BF16)


def outward(j, n):
    half = (j + 1) // 2
    return n // 2 + half - 2 * half * (j % 2)


def kernel(
    nl,
    ns,
    ny,
    near_ids_h,
    far_ids_h,
    top_ids_h,
    start_h,
    near_h,
    lb_h,
    lc_h,
    nt_h,
    bt_h,
    tc_h,
    basis_ref,
    hess_ref,
    near_ids,
    far_ids,
    top_ids,
    start_v,
    near_v,
    lb_v,
    lc_v,
    nt_v,
    bt_v,
    tc_v,
    t_v,
    tcw_v,
    gram_v,
    r1_0,
    r1_1,
    r1_2,
    r1_3,
    r2_0,
    r2_1,
    r2_2,
    r2_3,
    x_0,
    x_1,
    x_2,
    c_0,
    c_1,
    c_2,
    in_sem,
    r1_send,
    r1_recv,
    r2_send,
    r2_recv,
    x_send,
    x_recv,
    c_send,
    c_recv,
    g_send,
    g_recv,
):
    leaf, sub = lax.axis_index("leaf"), lax.axis_index("sub")
    r1, r2 = (r1_0, r1_1, r1_2, r1_3), (r2_0, r2_1, r2_2, r2_3)
    xall, call = (x_0, x_1, x_2), (c_0, c_1, c_2)
    nz = nl // ny
    z, y = leaf // ny, leaf % ny
    pairs = (
        (start_h, start_v),
        (bt_h, bt_v),
        (nt_h, nt_v),
        (lb_h, lb_v),
        (tc_h, tc_v),
        (lc_h, lc_v),
        (near_h, near_v),
        (near_ids_h, near_ids),
        (far_ids_h, far_ids),
        (top_ids_h, top_ids),
    )
    loads = [pltpu.make_async_copy(s, d, in_sem.at[i]) for i, (s, d) in enumerate(pairs)]

    columns = [lax.rem(y + outward(j, ny), ny) for j in range(ny)]

    def each_branch(act):
        def ring(j, c):
            row = lax.rem(z + outward(j, nz), nz) * ny
            for column in columns:
                act(row + column)
            return c

        lax.fori_loop(0, nz - 1, ring, 0)
        for column in columns[:-1]:
            act(z * ny + column)

    barrier = pltpu.get_barrier_semaphore()

    def greet_branch(to):
        pl.semaphore_signal(barrier, inc=1, device_id=(to, sub), device_id_type=MESH)

    def halo_at(j):
        side = j // ns
        back = 3 * (side // 2)
        to = lax.rem(leaf + side - back + nl, nl)
        return to, lax.rem(sub + j, ns), 1 - side + back

    def greet_halo(j, c):
        to, other, _ = halo_at(j)
        pl.semaphore_signal(barrier, inc=1, device_id=(to, other), device_id_type=MESH)
        return c

    each_branch(greet_branch)
    lax.fori_loop(1, 3 * ns, greet_halo, 0)
    for load in loads:
        load.start()

    row4 = lax.broadcasted_iota(jnp.int32, (4, 256), 0)
    row8 = lax.broadcasted_iota(jnp.int32, (8, 256), 0)
    lane = lax.broadcasted_iota(jnp.int32, (1, 128), 1)
    total = float(nl * ns * 4 * 256)

    for load in loads[:4]:
        load.wait()
    up = dot_nn(bt_v[0], nt_v[0]).astype(BF16)
    for leaf_i in range(4):
        t_v[:, 256 * leaf_i : 256 * (leaf_i + 1)] = dot_nn(
            up[:, 64 * leaf_i : 64 * (leaf_i + 1)], lb_v[leaf_i]
        ).astype(BF16)

    def fold(p):
        s = jnp.sum(p, axis=0, keepdims=True) * (1.0 / total)
        s = s[:, :128] + s[:, 128:]
        return s + pltpu.roll(s, 64, 1)

    def term_of(x8):
        x8f = x8.astype(F32)
        parts = [jnp.where(row8 % 4 == i, x8f, 0.0).astype(BF16) for i in range(4)]
        out = dot_nt(jnp.concatenate(parts, axis=1), t_v[...])
        out = jnp.sum(out, axis=0, keepdims=True)
        return jnp.concatenate([out, out], axis=1)

    def send_r1(k):
        def go(j, c):
            pltpu.make_async_remote_copy(
                r1[k].at[sub],
                r1[k].at[sub],
                r1_send.at[k],
                r1_recv.at[k],
                device_id=(leaf, lax.rem(sub + j, ns)),
                device_id_type=MESH,
            ).start()
            return c

        lax.fori_loop(1, ns, go, 0)

    def bytes_wait(ref, sem):
        pltpu.make_async_copy(ref, ref, sem).wait()

    def send_r2(k):
        def go(to):
            pltpu.make_async_remote_copy(
                r2[k].at[leaf],
                r2[k].at[leaf],
                r2_send.at[k],
                r2_recv.at[k],
                device_id=(to, sub),
                device_id_type=MESH,
            ).start()

        each_branch(go)

    def branch_sum(k):
        bytes_wait(r1[k].at[pl.ds(0, ns - 1)], r1_recv.at[k])
        sums = []
        for row in range(3):
            acc = r1[k][0, row]
            for j in range(1, ns):
                acc = acc + r1[k][j, row]
            sums.append(acc)
        return sums

    def send_gram():
        def go(j, c):
            pltpu.make_async_remote_copy(
                gram_v.at[sub],
                gram_v.at[sub],
                g_send,
                g_recv,
                device_id=(leaf, lax.rem(sub + j, ns)),
                device_id_type=MESH,
            ).start()
            return c

        lax.fori_loop(1, ns, go, 0)

    def send_x(k):
        def go(j, c):
            to, other, slot = halo_at(3 * ns - j)
            pltpu.make_async_remote_copy(
                xall[k].at[ns + sub],
                xall[k].at[slot * ns + sub],
                x_send.at[k],
                x_recv.at[k],
                device_id=(to, other),
                device_id_type=MESH,
            ).start()
            return c

        lax.fori_loop(1, 3 * ns, go, 0)

    def send_c(k):
        def go(j, c):
            pltpu.make_async_remote_copy(
                call[k].at[sub],
                call[k].at[sub],
                c_send.at[k],
                c_recv.at[k],
                device_id=(leaf, lax.rem(sub + j, ns)),
                device_id_type=MESH,
            ).start()
            return c

        lax.fori_loop(1, ns, go, 0)

    def store_coef(k, x8):
        out = dot_nt(x8, lb_v[...].reshape(256, 256))
        out = out[:4] + out[4:]
        for i in range(4):
            piece = out[i : i + 1, 128 * (i // 2) : 128 * (i // 2) + 128]
            piece = jnp.where((lane // 64) == i % 2, piece, 0.0)
            call[k][sub, i] = piece + pltpu.roll(piece, 64, 1)

    def own_part(x8):
        out = jnp.zeros((4, 256), F32)
        for i in range(4):
            o8 = dot_nt(x8, near_v[i, 0])
            out = jnp.where(row4 == i, o8[:4] + o8[4:], out)
        return out

    def partner_part(k):
        bytes_wait(xall[k].at[pl.ds(0, 3 * ns - 1)], x_recv.at[k])
        bytes_wait(call[k].at[pl.ds(0, ns - 1)], c_recv.at[k])
        near_rows, far_rows = [], []
        for i in range(4):
            one = near_ids[0, i]
            outside = jnp.logical_or(
                jnp.logical_and(leaf == 0, one < 4 * ns),
                jnp.logical_and(leaf == nl - 1, one >= 8 * ns),
            )
            keep = jnp.where(outside, 0.0, 1.0)
            near_rows.append(xall[k][one // 4, one % 4] * keep)
            first, second = far_ids[0, i], far_ids[1, i]
            far_rows.append(
                jnp.where(
                    lane < 64,
                    call[k][first // 4, first % 4],
                    call[k][second // 4, second % 4],
                )
            )
        p8 = split(jnp.concatenate(near_rows, axis=0))
        f8 = split(jnp.concatenate(far_rows, axis=0))
        out = jnp.zeros((4, 256), F32)
        for i in range(4):
            o8 = dot_nt(p8, near_v[i, 1])
            g8 = dot_nt(f8, lc_v[i])
            o4 = o8[:4] + o8[4:] + dot_nn((g8[:4] + g8[4:]).astype(BF16), lb_v[i])
            out = jnp.where(row4 == i, o4, out)
        return out

    def over_table(k, op):
        step = min(nl, 8)
        acc = None
        for c in range(0, nl, step):
            rows = r2[k][pl.ds(c, step)]
            part = jnp.max(jnp.abs(rows), axis=0) if op == "max" else jnp.sum(rows, axis=0)
            if acc is not None:
                part = jnp.maximum(acc, part) if op == "max" else acc + part
            acc = part
        return acc

    def half_sum(v, half):
        return jnp.sum(jnp.where((lane // 64) == half, v, 0.0), axis=1, keepdims=True)

    def exchange_leaves(k, x, x8):
        for i in range(4):
            xall[k][ns + sub, i] = x[i : i + 1]
        send_x(k)
        store_coef(k, x8)
        send_c(k)

    def leaves_sent(k):
        bytes_wait(xall[k].at[pl.ds(0, 3 * ns - 1)], x_send.at[k])
        bytes_wait(call[k].at[pl.ds(0, ns - 1)], c_send.at[k])

    low = lane < 64
    us = [start_v[...]]
    x8 = split(us[0])
    r1[0][sub, 0] = term_of(x8)
    r1[0][sub, 1] = fold(us[0] * us[0])
    r1[0][sub, 2] = jnp.zeros((1, 128), F32)
    pl.semaphore_wait(barrier, nl - 1 + 3 * ns - 1)
    send_r1(0)
    exchange_leaves(0, us[0], x8)
    both = dot_nt(t_v[...], t_v[...])
    gram_v[sub] = jnp.concatenate([both, both], axis=1)
    order = [(i, j) for i in range(4) for j in range(i + 1)]
    pending = jnp.zeros((1, 128), F32)

    def put(row, i, j, value):
        return row + jnp.where(lane == order.index((i, j)), value, 0.0)

    sums = branch_sum(0)
    r2[0][leaf] = sums[0]
    send_r2(0)
    send_gram()
    pending = put(pending, 0, 0, half_sum(sums[1], 0))
    branchc = [sums[0]]
    for load in loads[4:]:
        load.wait()
    before = jnp.ones((1, 1), F32)
    nus = []
    own = own_part(x8)
    for k in range(STEPS):
        local = own + partner_part(k)
        r1[k + 1][sub, 0] = term_of(split(local))
        dots = [fold(local * u) for u in us]
        r1[k + 1][sub, 1] = jnp.where(low, fold(local * local), dots[0])
        r1[k + 1][sub, 2] = jnp.where(low, dots[min(k, 1)], dots[k])
        send_r1(k + 1)
        if k == 0:
            bytes_wait(gram_v.at[pl.ds(0, ns - 1)], g_recv)
            whole = gram_v[0]
            for j in range(1, ns):
                whole = whole + gram_v[j]
            both = dot_nn(whole[:, :64].astype(BF16), tc_v[0]).astype(BF16)
            tcw_v[:64] = both
            tcw_v[64:128] = both
            tcw_v[128:192] = tc_v[0]
            tcw_v[192:] = tc_v[0]
        sums = branch_sum(k + 1)
        bytes_wait(r2[k].at[pl.ds(0, nl - 1)], r2_recv.at[k])
        picked = [r2[k][top_ids[0, s]] for s in range(4)]
        pair0 = jnp.where(low, picked[0], picked[1])
        pair1 = jnp.where(low, picked[2], picked[3])
        chosen = split(jnp.concatenate([pair0, pair1], axis=1))
        got = dot_nt(chosen, tcw_v[...])
        got = (got[:1] + got[1:]) * before
        added, branchl = got[:, :128], got[:, 128:]
        if k < 2:
            later = sums[0] + added
            r2[k + 1][leaf] = later
            send_r2(k + 1)
            biggest = jnp.max(over_table(k, "max"), axis=1, keepdims=True) * before
            alpha = 1.0 / jnp.maximum(biggest, 1.0)
        else:
            alpha = jnp.full((1, 1), 2.0**-20, F32)
        nus.append(1.0 / alpha)
        def inner_products(row):
            scaled = branchl * (alpha * (1.0 / total))
            factors = jnp.where(low, alpha * (2.0 * sums[0] + added), branchc[0])
            first = sums[1] * jnp.where(low, alpha * alpha, alpha) + scaled * factors
            row = put(row, k + 1, k + 1, half_sum(first, 0))
            row = put(row, k + 1, 0, half_sum(first, 1))
            if k >= 1:
                second = sums[2] * alpha + scaled * jnp.where(low, branchc[1], branchc[k])
                row = put(row, k + 1, 1, half_sum(second, 0))
                if k == 2:
                    row = put(row, 3, 2, half_sum(second, 1))
            return row

        if k == 2:
            r2[3][leaf] = inner_products(pending)
            send_r2(3)
        down = jnp.sum(dot_nn(split(branchl[:, :64]), t_v[...]), axis=0, keepdims=True)
        down = jnp.concatenate([down[:, 256 * i : 256 * (i + 1)] for i in range(4)], axis=0)
        x = (local + down) * alpha
        us.append(x)
        if k < 2:
            x8 = split(x)
            exchange_leaves(k + 1, x, x8)
            own = own_part(x8)
            pending = inner_products(pending)
            branchc.append(later * alpha)
            before = alpha

    bytes_wait(r2[3].at[pl.ds(0, nl - 1)], r2_recv.at[3])
    sums = over_table(3, "sum")
    gram = {ij: sums[:, i : i + 1] for i, ij in enumerate(order)}

    def g(i, j):
        return gram[max(i, j), min(i, j)]

    zero = jnp.zeros((1, 1), F32)
    coefs = [[lax.rsqrt(gram[0, 0] + 1e-06)]]
    basis_ref[0] = us[0] * coefs[0][0]
    hess = {}

    def column(j):
        a = coefs[j]
        w = []
        for i in range(j + 2):
            v = zero
            if i <= j:
                v = v + 0.5 * a[i]
            if i >= 1:
                v = v + nus[i - 1] * a[i - 1]
            w.append(v)
        gw = [sum((g(i, m) * w[m] for m in range(1, j + 2)), g(i, 0) * w[0]) for i in range(j + 2)]
        square = sum((w[i] * gw[i] for i in range(1, j + 2)), w[0] * gw[0])
        remain = square
        new = list(w)
        for i in range(j + 1):
            h = sum((coefs[i][m] * gw[m] for m in range(1, i + 1)), coefs[i][0] * gw[0])
            hess[i, j] = h
            remain = remain - h * h
            for m in range(i + 1):
                new[m] = new[m] - h * coefs[i][m]
        scale = jnp.sqrt(jnp.maximum(remain, 0.01 * square))
        hess[j + 1, j] = scale
        inverse = 1.0 / scale
        coefs.append([v * inverse for v in new])

    def store_basis(j):
        acc = us[0] * coefs[j][0]
        for m in range(1, j + 1):
            acc = acc + us[m] * coefs[j][m]
        basis_ref[j] = acc

    for j in range(STEPS):
        column(j)
        store_basis(j + 1)
    rows = lax.broadcasted_iota(jnp.int32, (4, 3), 0)
    cols = lax.broadcasted_iota(jnp.int32, (4, 3), 1)
    table = jnp.zeros((4, 3), F32)
    for (i, j), h in hess.items():
        table = jnp.where(jnp.logical_and(rows == i, cols == j), h, table)
    hess_ref[...] = table

    for k in range(4):
        bytes_wait(r1[k].at[pl.ds(0, ns - 1)], r1_send.at[k])
        bytes_wait(r2[k].at[pl.ds(0, nl - 1)], r2_send.at[k])
    for k in range(STEPS):
        leaves_sent(k)
    bytes_wait(gram_v.at[pl.ds(0, ns - 1)], g_send)


def solution(mesh):
    nl, ns = mesh.shape["leaf"], mesh.shape["sub"]
    ny = RING if nl % RING == 0 else 1

    def per_device(
        start_vec,
        near_blocks,
        near_ids,
        far_ids,
        leaf_basis,
        leaf_coupling,
        node_transfer,
        branch_transfer,
        top_ids,
        top_coupling,
    ):
        hbm = pl.BlockSpec(memory_space=pltpu.HBM)
        vmem = pl.BlockSpec(memory_space=pltpu.VMEM)
        dma = pltpu.SemaphoreType.DMA
        return pl.pallas_call(
            functools.partial(kernel, nl, ns, ny),
            out_shape=(
                jax.ShapeDtypeStruct((4, 4, 256), F32),
                jax.ShapeDtypeStruct((4, 3), F32),
            ),
            in_specs=[hbm] * 10,
            out_specs=(vmem, vmem),
            scratch_shapes=[
                pltpu.SMEM((1, 4), jnp.int32),
                pltpu.SMEM((2, 4), jnp.int32),
                pltpu.SMEM((1, 4), jnp.int32),
                pltpu.VMEM((4, 256), F32),
                pltpu.VMEM((4, 2, 256, 256), BF16),
                pltpu.VMEM((4, 64, 256), BF16),
                pltpu.VMEM((4, 64, 128), BF16),
                pltpu.VMEM((1, 64, 256), BF16),
                pltpu.VMEM((1, 64, 64), BF16),
                pltpu.VMEM((1, 64, 256), BF16),
                pltpu.VMEM((64, 1024), BF16),
                pltpu.VMEM((256, 256), BF16),
                pltpu.VMEM((ns, 64, 128), F32),
                *[pltpu.VMEM((ns, 3, 1, 128), F32)] * 4,
                *[pltpu.VMEM((nl, 1, 128), F32)] * 4,
                *[pltpu.VMEM((3 * ns, 4, 1, 256), F32)] * 3,
                *[pltpu.VMEM((ns, 4, 1, 128), F32)] * 3,
                dma((10,)),
                dma((4,)),
                dma((4,)),
                dma((4,)),
                dma((4,)),
                dma((3,)),
                dma((3,)),
                dma((3,)),
                dma((3,)),
                dma,
                dma,
            ],
            compiler_params=pltpu.CompilerParams(
                collective_id=0, has_side_effects=True, vmem_limit_bytes=40 * 2**20
            ),
        )(
            *(
                pltpu.with_memory_space_constraint(v, pltpu.HBM)
                for v in (
                    near_ids.T,
                    far_ids.T,
                    top_ids,
                    start_vec,
                    near_blocks,
                    leaf_basis,
                    leaf_coupling,
                    node_transfer,
                    branch_transfer,
                    top_coupling,
                )
            )
        )

    placed = (
        P(("leaf", "sub"), None),
        P(("leaf", "sub"), None, None, None),
        P(("leaf", "sub"), None),
        P(("leaf", "sub"), None),
        P(("leaf", "sub"), None, None),
        P(("leaf", "sub"), None, None),
        P(("leaf", "sub"), None, None),
        P(("leaf", "sub"), None, None),
        P("leaf", None),
        P("leaf", None, None),
    )
    return jax.shard_map(
        per_device,
        mesh=mesh,
        in_specs=placed,
        out_specs=(P(None, ("leaf", "sub"), None), P()),
        check_vma=False,
    )
```

```python
import functools

import jax
import jax.numpy as jnp
from jax import lax
from jax.experimental import pallas as pl
from jax.experimental.pallas import tpu as pltpu
from jax.sharding import PartitionSpec as P

MESH = pl.DeviceIdType.MESH
F32 = jnp.float32
BF16 = jnp.bfloat16
STEPS = 3
RING = 8


def dot_nt(a, b):
    return lax.dot_general(a, b, (((1,), (1,)), ((), ())), preferred_element_type=F32)


def dot_nn(a, b):
    return lax.dot_general(a, b, (((1,), (0,)), ((), ())), preferred_element_type=F32)


def split(x):
    high = x.astype(BF16).astype(F32)
    return jnp.concatenate([high, x - high], axis=0).astype(BF16)


def outward(j, n):
    half = (j + 1) // 2
    return n // 2 + half - 2 * half * (j % 2)


def kernel(
    nl,
    ns,
    ny,
    near_ids_h,
    far_ids_h,
    top_ids_h,
    start_h,
    near_h,
    lb_h,
    lc_h,
    nt_h,
    bt_h,
    tc_h,
    basis_ref,
    hess_ref,
    near_ids,
    far_ids,
    top_ids,
    start_v,
    near_v,
    lb_v,
    lc_v,
    nt_v,
    bt_v,
    tc_v,
    t_v,
    tcw_v,
    gram_v,
    r1_0,
    r1_1,
    r1_2,
    r1_3,
    r2_0,
    r2_1,
    r2_2,
    r2_3,
    x_0,
    x_1,
    x_2,
    c_0,
    c_1,
    c_2,
    in_sem,
    r1_send,
    r1_recv,
    r2_send,
    r2_recv,
    x_send,
    x_recv,
    c_send,
    c_recv,
    g_send,
    g_recv,
):
    leaf, sub = lax.axis_index("leaf"), lax.axis_index("sub")
    r1, r2 = (r1_0, r1_1, r1_2, r1_3), (r2_0, r2_1, r2_2, r2_3)
    xall, call = (x_0, x_1, x_2), (c_0, c_1, c_2)
    nz = nl // ny
    z, y = leaf // ny, leaf % ny
    pairs = (
        (start_h, start_v),
        (bt_h, bt_v),
        (nt_h, nt_v),
        (lb_h, lb_v),
        (tc_h, tc_v),
        (lc_h, lc_v),
        (near_h, near_v),
        (near_ids_h, near_ids),
        (far_ids_h, far_ids),
        (top_ids_h, top_ids),
    )
    loads = [pltpu.make_async_copy(s, d, in_sem.at[i]) for i, (s, d) in enumerate(pairs)]
    for load in loads:
        load.start()

    columns = [lax.rem(y + outward(j, ny), ny) for j in range(ny)]

    def each_branch(act):
        def ring(j, c):
            row = lax.rem(z + outward(j, nz), nz) * ny
            for column in columns:
                act(row + column)
            return c

        lax.fori_loop(0, nz - 1, ring, 0)
        for column in columns[:-1]:
            act(z * ny + column)

    barrier = pltpu.get_barrier_semaphore()

    def greet_branch(to):
        pl.semaphore_signal(barrier, inc=1, device_id=(to, sub), device_id_type=MESH)

    def halo_at(j):
        side = j // ns
        back = 3 * (side // 2)
        to = lax.rem(leaf + side - back + nl, nl)
        return to, lax.rem(sub + j, ns), 1 - side + back

    def greet_halo(j, c):
        to, other, _ = halo_at(j)
        pl.semaphore_signal(barrier, inc=1, device_id=(to, other), device_id_type=MESH)
        return c

    each_branch(greet_branch)
    lax.fori_loop(1, 3 * ns, greet_halo, 0)

    row4 = lax.broadcasted_iota(jnp.int32, (4, 256), 0)
    row8 = lax.broadcasted_iota(jnp.int32, (8, 256), 0)
    lane = lax.broadcasted_iota(jnp.int32, (1, 128), 1)
    total = float(nl * ns * 4 * 256)

    for load in loads[:4]:
        load.wait()
    up = dot_nn(bt_v[0], nt_v[0]).astype(BF16)
    for leaf_i in range(4):
        t_v[:, 256 * leaf_i : 256 * (leaf_i + 1)] = dot_nn(
            up[:, 64 * leaf_i : 64 * (leaf_i + 1)], lb_v[leaf_i]
        ).astype(BF16)

    def fold(p):
        s = jnp.sum(p, axis=0, keepdims=True) * (1.0 / total)
        s = s[:, :128] + s[:, 128:]
        return s + pltpu.roll(s, 64, 1)

    def term_of(x8):
        x8f = x8.astype(F32)
        parts = [jnp.where(row8 % 4 == i, x8f, 0.0).astype(BF16) for i in range(4)]
        out = dot_nt(jnp.concatenate(parts, axis=1), t_v[...])
        out = jnp.sum(out, axis=0, keepdims=True)
        return jnp.concatenate([out, out], axis=1)

    def send_r1(k):
        def go(j, c):
            pltpu.make_async_remote_copy(
                r1[k].at[sub],
                r1[k].at[sub],
                r1_send.at[k],
                r1_recv.at[k],
                device_id=(leaf, lax.rem(sub + j, ns)),
                device_id_type=MESH,
            ).start()
            return c

        lax.fori_loop(1, ns, go, 0)

    def bytes_wait(ref, sem):
        pltpu.make_async_copy(ref, ref, sem).wait()

    def send_r2(k):
        def go(to):
            pltpu.make_async_remote_copy(
                r2[k].at[leaf],
                r2[k].at[leaf],
                r2_send.at[k],
                r2_recv.at[k],
                device_id=(to, sub),
                device_id_type=MESH,
            ).start()

        each_branch(go)

    def branch_sum(k):
        bytes_wait(r1[k].at[pl.ds(0, ns - 1)], r1_recv.at[k])
        sums = []
        for row in range(3):
            acc = r1[k][0, row]
            for j in range(1, ns):
                acc = acc + r1[k][j, row]
            sums.append(acc)
        return sums

    def send_gram():
        def go(j, c):
            pltpu.make_async_remote_copy(
                gram_v.at[sub],
                gram_v.at[sub],
                g_send,
                g_recv,
                device_id=(leaf, lax.rem(sub + j, ns)),
                device_id_type=MESH,
            ).start()
            return c

        lax.fori_loop(1, ns, go, 0)

    def send_x(k):
        def go(j, c):
            to, other, slot = halo_at(j)
            pltpu.make_async_remote_copy(
                xall[k].at[ns + sub],
                xall[k].at[slot * ns + sub],
                x_send.at[k],
                x_recv.at[k],
                device_id=(to, other),
                device_id_type=MESH,
            ).start()
            return c

        lax.fori_loop(1, 3 * ns, go, 0)

    def send_c(k):
        def go(j, c):
            pltpu.make_async_remote_copy(
                call[k].at[sub],
                call[k].at[sub],
                c_send.at[k],
                c_recv.at[k],
                device_id=(leaf, lax.rem(sub + j, ns)),
                device_id_type=MESH,
            ).start()
            return c

        lax.fori_loop(1, ns, go, 0)

    def store_coef(k, x8):
        out = dot_nt(x8, lb_v[...].reshape(256, 256))
        out = out[:4] + out[4:]
        for i in range(4):
            piece = out[i : i + 1, 128 * (i // 2) : 128 * (i // 2) + 128]
            piece = jnp.where((lane // 64) == i % 2, piece, 0.0)
            call[k][sub, i] = piece + pltpu.roll(piece, 64, 1)

    def own_part(x8):
        out = jnp.zeros((4, 256), F32)
        for i in range(4):
            o8 = dot_nt(x8, near_v[i, 0])
            out = jnp.where(row4 == i, o8[:4] + o8[4:], out)
        return out

    def partner_part(k):
        bytes_wait(xall[k].at[pl.ds(0, 3 * ns - 1)], x_recv.at[k])
        near_rows, far_rows = [], []
        for i in range(4):
            one = near_ids[0, i]
            outside = jnp.logical_or(
                jnp.logical_and(leaf == 0, one < 4 * ns),
                jnp.logical_and(leaf == nl - 1, one >= 8 * ns),
            )
            keep = jnp.where(outside, 0.0, 1.0)
            near_rows.append(xall[k][one // 4, one % 4] * keep)
        p8 = split(jnp.concatenate(near_rows, axis=0))
        out = jnp.zeros((4, 256), F32)
        for i in range(4):
            o8 = dot_nt(p8, near_v[i, 1])
            out = jnp.where(row4 == i, o8[:4] + o8[4:], out)
        bytes_wait(call[k].at[pl.ds(0, ns - 1)], c_recv.at[k])
        for i in range(4):
            first, second = far_ids[0, i], far_ids[1, i]
            far_rows.append(
                jnp.where(
                    lane < 64,
                    call[k][first // 4, first % 4],
                    call[k][second // 4, second % 4],
                )
            )
        f8 = split(jnp.concatenate(far_rows, axis=0))
        for i in range(4):
            g8 = dot_nt(f8, lc_v[i])
            o4 = dot_nn((g8[:4] + g8[4:]).astype(BF16), lb_v[i])
            out = jnp.where(row4 == i, out + o4, out)
        return out

    def over_table(k, op):
        step = min(nl, 8)
        acc = None
        for c in range(0, nl, step):
            rows = r2[k][pl.ds(c, step)]
            part = jnp.max(jnp.abs(rows), axis=0) if op == "max" else jnp.sum(rows, axis=0)
            if acc is not None:
                part = jnp.maximum(acc, part) if op == "max" else acc + part
            acc = part
        return acc

    def half_sum(v, half):
        return jnp.sum(jnp.where((lane // 64) == half, v, 0.0), axis=1, keepdims=True)

    def exchange_leaves(k, x, x8):
        for i in range(4):
            xall[k][ns + sub, i] = x[i : i + 1]
        send_x(k)
        store_coef(k, x8)
        send_c(k)

    def leaves_sent(k):
        bytes_wait(xall[k].at[pl.ds(0, 3 * ns - 1)], x_send.at[k])
        bytes_wait(call[k].at[pl.ds(0, ns - 1)], c_send.at[k])

    low = lane < 64
    us = [start_v[...]]
    x8 = split(us[0])
    r1[0][sub, 0] = term_of(x8)
    r1[0][sub, 1] = fold(us[0] * us[0])
    r1[0][sub, 2] = jnp.zeros((1, 128), F32)
    pl.semaphore_wait(barrier, nl - 1 + 3 * ns - 1)
    send_r1(0)
    exchange_leaves(0, us[0], x8)
    both = dot_nt(t_v[...], t_v[...])
    gram_v[sub] = jnp.concatenate([both, both], axis=1)
    order = [(i, j) for i in range(4) for j in range(i + 1)]
    pending = jnp.zeros((1, 128), F32)

    def put(row, i, j, value):
        return row + jnp.where(lane == order.index((i, j)), value, 0.0)

    sums = branch_sum(0)
    r2[0][leaf] = sums[0]
    send_r2(0)
    send_gram()
    pending = put(pending, 0, 0, half_sum(sums[1], 0))
    branchc = [sums[0]]
    for load in loads[4:]:
        load.wait()
    before = jnp.ones((1, 1), F32)
    nus = []
    own = own_part(x8)
    for k in range(STEPS):
        local = own + partner_part(k)
        r1[k + 1][sub, 0] = term_of(split(local))
        dots = [fold(local * u) for u in us]
        r1[k + 1][sub, 1] = jnp.where(low, fold(local * local), dots[0])
        r1[k + 1][sub, 2] = jnp.where(low, dots[min(k, 1)], dots[k])
        send_r1(k + 1)
        if k == 0:
            bytes_wait(gram_v.at[pl.ds(0, ns - 1)], g_recv)
            whole = gram_v[0]
            for j in range(1, ns):
                whole = whole + gram_v[j]
            both = dot_nn(whole[:, :64].astype(BF16), tc_v[0]).astype(BF16)
            tcw_v[:64] = both
            tcw_v[64:128] = both
            tcw_v[128:192] = tc_v[0]
            tcw_v[192:] = tc_v[0]
        sums = branch_sum(k + 1)
        bytes_wait(r2[k].at[pl.ds(0, nl - 1)], r2_recv.at[k])
        picked = [r2[k][top_ids[0, s]] for s in range(4)]
        pair0 = jnp.where(low, picked[0], picked[1])
        pair1 = jnp.where(low, picked[2], picked[3])
        chosen = split(jnp.concatenate([pair0, pair1], axis=1))
        got = dot_nt(chosen, tcw_v[...])
        got = (got[:1] + got[1:]) * before
        added, branchl = got[:, :128], got[:, 128:]
        if k < 2:
            later = sums[0] + added
            r2[k + 1][leaf] = later
            send_r2(k + 1)
            biggest = jnp.max(over_table(k, "max"), axis=1, keepdims=True) * before
            alpha = 1.0 / jnp.maximum(biggest, 1.0)
        else:
            alpha = jnp.full((1, 1), 2.0**-20, F32)
        nus.append(1.0 / alpha)
        scaled = branchl * (alpha * (1.0 / total))
        factors = jnp.where(low, alpha * (2.0 * sums[0] + added), branchc[0])
        first = sums[1] * jnp.where(low, alpha * alpha, alpha) + scaled * factors
        pending = put(pending, k + 1, k + 1, half_sum(first, 0))
        pending = put(pending, k + 1, 0, half_sum(first, 1))
        if k >= 1:
            second = sums[2] * alpha + scaled * jnp.where(low, branchc[1], branchc[k])
            pending = put(pending, k + 1, 1, half_sum(second, 0))
            if k == 2:
                pending = put(pending, 3, 2, half_sum(second, 1))
        if k == 2:
            r2[3][leaf] = pending
            send_r2(3)
        down = jnp.sum(dot_nn(split(branchl[:, :64]), t_v[...]), axis=0, keepdims=True)
        down = jnp.concatenate([down[:, 256 * i : 256 * (i + 1)] for i in range(4)], axis=0)
        x = (local + down) * alpha
        us.append(x)
        if k < 2:
            x8 = split(x)
            exchange_leaves(k + 1, x, x8)
            branchc.append(later * alpha)
            before = alpha
            own = own_part(x8)

    bytes_wait(r2[3].at[pl.ds(0, nl - 1)], r2_recv.at[3])
    sums = over_table(3, "sum")
    gram = {ij: sums[:, i : i + 1] for i, ij in enumerate(order)}

    def g(i, j):
        return gram[max(i, j), min(i, j)]

    zero = jnp.zeros((1, 1), F32)
    coefs = [[lax.rsqrt(gram[0, 0] + 1e-06)]]
    basis_ref[0] = us[0] * coefs[0][0]
    hess = {}

    def column(j):
        a = coefs[j]
        w = []
        for i in range(j + 2):
            v = zero
            if i <= j:
                v = v + 0.5 * a[i]
            if i >= 1:
                v = v + nus[i - 1] * a[i - 1]
            w.append(v)
        gw = [sum((g(i, m) * w[m] for m in range(1, j + 2)), g(i, 0) * w[0]) for i in range(j + 2)]
        square = sum((w[i] * gw[i] for i in range(1, j + 2)), w[0] * gw[0])
        remain = square
        new = list(w)
        for i in range(j + 1):
            h = sum((coefs[i][m] * gw[m] for m in range(1, i + 1)), coefs[i][0] * gw[0])
            hess[i, j] = h
            remain = remain - h * h
            for m in range(i + 1):
                new[m] = new[m] - h * coefs[i][m]
        scale = jnp.sqrt(jnp.maximum(remain, 0.01 * square))
        hess[j + 1, j] = scale
        inverse = 1.0 / scale
        coefs.append([v * inverse for v in new])

    def store_basis(j):
        acc = us[0] * coefs[j][0]
        for m in range(1, j + 1):
            acc = acc + us[m] * coefs[j][m]
        basis_ref[j] = acc

    for j in range(STEPS):
        column(j)
        store_basis(j + 1)
    rows = lax.broadcasted_iota(jnp.int32, (4, 3), 0)
    cols = lax.broadcasted_iota(jnp.int32, (4, 3), 1)
    table = jnp.zeros((4, 3), F32)
    for (i, j), h in hess.items():
        table = jnp.where(jnp.logical_and(rows == i, cols == j), h, table)
    hess_ref[...] = table

    for k in range(4):
        bytes_wait(r1[k].at[pl.ds(0, ns - 1)], r1_send.at[k])
        bytes_wait(r2[k].at[pl.ds(0, nl - 1)], r2_send.at[k])
    for k in range(STEPS):
        leaves_sent(k)
    bytes_wait(gram_v.at[pl.ds(0, ns - 1)], g_send)


def solution(mesh):
    nl, ns = mesh.shape["leaf"], mesh.shape["sub"]
    ny = RING if nl % RING == 0 else 1

    def per_device(
        start_vec,
        near_blocks,
        near_ids,
        far_ids,
        leaf_basis,
        leaf_coupling,
        node_transfer,
        branch_transfer,
        top_ids,
        top_coupling,
    ):
        hbm = pl.BlockSpec(memory_space=pltpu.HBM)
        vmem = pl.BlockSpec(memory_space=pltpu.VMEM)
        dma = pltpu.SemaphoreType.DMA
        return pl.pallas_call(
            functools.partial(kernel, nl, ns, ny),
            out_shape=(
                jax.ShapeDtypeStruct((4, 4, 256), F32),
                jax.ShapeDtypeStruct((4, 3), F32),
            ),
            in_specs=[hbm] * 10,
            out_specs=(vmem, vmem),
            scratch_shapes=[
                pltpu.SMEM((1, 4), jnp.int32),
                pltpu.SMEM((2, 4), jnp.int32),
                pltpu.SMEM((1, 4), jnp.int32),
                pltpu.VMEM((4, 256), F32),
                pltpu.VMEM((4, 2, 256, 256), BF16),
                pltpu.VMEM((4, 64, 256), BF16),
                pltpu.VMEM((4, 64, 128), BF16),
                pltpu.VMEM((1, 64, 256), BF16),
                pltpu.VMEM((1, 64, 64), BF16),
                pltpu.VMEM((1, 64, 256), BF16),
                pltpu.VMEM((64, 1024), BF16),
                pltpu.VMEM((256, 256), BF16),
                pltpu.VMEM((ns, 64, 128), F32),
                *[pltpu.VMEM((ns, 3, 1, 128), F32)] * 4,
                *[pltpu.VMEM((nl, 1, 128), F32)] * 4,
                *[pltpu.VMEM((3 * ns, 4, 1, 256), F32)] * 3,
                *[pltpu.VMEM((ns, 4, 1, 128), F32)] * 3,
                dma((10,)),
                dma((4,)),
                dma((4,)),
                dma((4,)),
                dma((4,)),
                dma((3,)),
                dma((3,)),
                dma((3,)),
                dma((3,)),
                dma,
                dma,
            ],
            compiler_params=pltpu.CompilerParams(
                collective_id=0, has_side_effects=True, vmem_limit_bytes=40 * 2**20
            ),
        )(
            *(
                pltpu.with_memory_space_constraint(v, pltpu.HBM)
                for v in (
                    near_ids.T,
                    far_ids.T,
                    top_ids,
                    start_vec,
                    near_blocks,
                    leaf_basis,
                    leaf_coupling,
                    node_transfer,
                    branch_transfer,
                    top_coupling,
                )
            )
        )

    placed = (
        P(("leaf", "sub"), None),
        P(("leaf", "sub"), None, None, None),
        P(("leaf", "sub"), None),
        P(("leaf", "sub"), None),
        P(("leaf", "sub"), None, None),
        P(("leaf", "sub"), None, None),
        P(("leaf", "sub"), None, None),
        P(("leaf", "sub"), None, None),
        P("leaf", None),
        P("leaf", None, None),
    )
    return jax.shard_map(
        per_device,
        mesh=mesh,
        in_specs=placed,
        out_specs=(P(None, ("leaf", "sub"), None), P()),
        check_vma=False,
    )
```
